256 devices in a mesh: kq: 128 (over x, y, z), band: 2 (over core).
Axes of the slice: x: 4, y: 4, z: 8, core: 2. Of those that a mesh axis runs over, the one named last changes fastest.
Arguments:
- orbitals: bfloat16 [128, 16, 4096], P('kq', 'band'), may hold values from -6 to 6
- screening: bfloat16 [256, 1024, 1024], P('kq'), may hold values from -0.1875 to 0.1875
- pair_k: int32 [256, 2], replicated, may hold values from 0 to 127, as said below
- pair_q: int32 [256], P('kq'), may hold values from 0 to 255, as said below
- gmap: int32 [1024], replicated, may hold values from 0 to 4095, as said below
Outputs:
- exch_field: float32 [128, 16, 4096], P('kq', 'band')
The draws below stay inside these ranges and needn't reach their ends.
Inputs may be any that keep to these rules, and one draw needn't show every extreme that they name: Rows are grouped by owner: rows o * 2 to (o + 1) * 2 - 1 belong to kq index o, and pair_k[o * 2 + i, s] = (pair_k[i, s] + o) mod 128 for every row i of owner 0 and both columns s. The 2 * 2 k-points of one owner are all different, and those of owner 0 include 128 - 1 and 64. `pair_q`: row i names one of the 2 transfers of owner o = i // 2, namely 2 * o to 2 * o + 1, and each of them in 1 of the owner's rows. `gmap`: all entries differ; 0 and 4095 are among them.
All inputs are finite; a program needn't handle non-finite values.
Results may differ from the reference program's by a relative error of at most 0.007.
Values may be sent and summed in bfloat16 or wider, within the bound.
A program may use at most 128 MiB of HBM per device.

```python
import math
import jax
import jax.numpy as jnp
from jax import lax

GRID = 16
R = 4096
NG = 1024
NB = 16
Q_DEV = 2
P_DEV = 2
NK = 128
NQ = 256
PAIRS = 256


def draw_pair_k(key, part):
    rest = jax.random.permutation(jax.random.fold_in(key, 11), NK - 2)[:2 * P_DEV - 2].astype(jnp.int32)
    rest = rest + (rest >= NK // 2).astype(jnp.int32)
    fixed_pair = jnp.array([NK - 1, NK // 2], jnp.int32)
    listed = jnp.concatenate([fixed_pair, rest])
    order = jax.random.permutation(jax.random.fold_in(key, 13), 2 * P_DEV)
    offsets = listed[order].astype(jnp.int32)
    owners = jnp.arange(NK, dtype=jnp.int32)
    refs = (owners[:, None] + offsets[None, :]) % NK
    first_points = refs[:, :P_DEV].reshape(PAIRS)
    second_points = refs[:, P_DEV:].reshape(PAIRS)
    return jnp.stack([first_points, second_points], axis=1).astype(jnp.int32)


def draw_pair_q(key, part):
    shifts = jax.random.randint(jax.random.fold_in(key, 23), (NK, 1), 0, Q_DEV).astype(jnp.int32)
    owners = jnp.arange(NK, dtype=jnp.int32)[:, None]
    within = jnp.arange(P_DEV, dtype=jnp.int32)[None, :]
    return (owners * Q_DEV + (within + shifts) % Q_DEV).reshape(PAIRS).astype(jnp.int32)


def draw_gmap(key, part):
    inner = jax.random.permutation(jax.random.fold_in(key, 31), GRID ** 3 - 2)[:NG - 2].astype(jnp.int32) + 1
    listed = jnp.concatenate([jnp.array([0, GRID ** 3 - 1], jnp.int32), inner])
    order = jax.random.permutation(jax.random.fold_in(key, 37), NG)
    return listed[order].astype(jnp.int32)


def level_of(own_key, extent, cuts, least, largest):
    level, own = 1.0, jax.random.fold_in(own_key, 6)
    for position, shards_of in cuts:
        draws = jnp.exp(jax.random.uniform(jax.random.fold_in(own, position), (shards_of,), jnp.float32, least / len(cuts), largest / len(cuts)))
        level = level * jnp.repeat(draws, extent[position] // shards_of).reshape([-1 if axis == position else 1 for axis in range(len(extent))])
    return level


def noise(rng, shape, spread, most, split=(), held_as=jnp.bfloat16):
    values = spread * jax.random.normal(rng, shape, jnp.float32)
    if split:
        values = values * level_of(rng, shape, split, -0.22, 0.18)
    return jnp.clip(values, -most, most).astype(held_as)


def setup_inputs(seed: int = 0) -> dict:
    key_list = jax.random.split(jax.random.key(seed), 6)
    orbitals = noise(key_list[0], (NK, NB, R), 1.0, 6.0, ((0, 128), (1, 2)))
    screening = noise(key_list[1], (NQ, NG, NG), NG ** -0.5, 0.1875, ((0, 128),))
    pair_k = draw_pair_k(jax.random.fold_in(key_list[5], 71), 0)
    pair_q = draw_pair_q(jax.random.fold_in(key_list[5], 71), 0)
    gmap = draw_gmap(jax.random.fold_in(key_list[5], 71), 0)
    return dict(orbitals=orbitals, screening=screening, pair_k=pair_k, pair_q=pair_q, gmap=gmap)


def cas_table(gmap, grid_side):
    cells = grid_side ** 3
    points = jnp.arange(cells, dtype=jnp.int32)
    coord_x = points // (grid_side * grid_side)
    coord_y = points // grid_side % grid_side
    coord_z = points % grid_side
    freq_x = gmap // (grid_side * grid_side)
    freq_y = gmap // grid_side % grid_side
    freq_z = gmap % grid_side
    phase = (freq_x[:, None] * coord_x[None, :] + freq_y[:, None] * coord_y[None, :] + freq_z[:, None] * coord_z[None, :]) % grid_side
    angle = phase.astype(jnp.float32) * (2.0 * math.pi / grid_side)
    return (jnp.cos(angle) + jnp.sin(angle)).astype(jnp.bfloat16)

def pair_fields(left_block, right_block, screen_mat, table):
    rows_left = left_block.shape[0]
    rows_right = right_block.shape[0]
    cells = table.shape[1]
    factor = 1.0 / math.sqrt(cells)
    density = (left_block.astype(jnp.float32)[:, None, :] * right_block.astype(jnp.float32)[None, :, :]).astype(jnp.bfloat16)
    density = density.reshape(rows_left * rows_right, cells)
    table32 = table.astype(jnp.float32)
    spectrum = (jnp.dot(density.astype(jnp.float32), table32.T, preferred_element_type=jnp.float32) * factor).astype(jnp.bfloat16)
    screened = jnp.dot(spectrum.astype(jnp.float32), screen_mat.astype(jnp.float32), preferred_element_type=jnp.float32).astype(jnp.bfloat16)
    potential = (jnp.dot(screened.astype(jnp.float32), table32, preferred_element_type=jnp.float32) * factor).astype(jnp.bfloat16)
    potential = potential.reshape(rows_left, rows_right, cells).astype(jnp.float32)
    toward_left = jnp.einsum('mnr,nr->mr', potential, right_block.astype(jnp.float32))
    toward_right = jnp.einsum('mnr,mr->nr', potential, left_block.astype(jnp.float32))
    return (toward_left, toward_right)

def reference(orbitals, screening, pair_k, pair_q, gmap):
    table = cas_table(gmap, GRID)

    def accumulate(index, totals):
        first_point = pair_k[index, 0]
        second_point = pair_k[index, 1]
        transfer = pair_q[index]
        left_block = lax.dynamic_index_in_dim(orbitals, first_point, 0, keepdims=False)
        right_block = lax.dynamic_index_in_dim(orbitals, second_point, 0, keepdims=False)
        screen_mat = lax.dynamic_index_in_dim(screening, transfer, 0, keepdims=False)
        toward_left, toward_right = pair_fields(left_block, right_block, screen_mat, table)
        totals = totals.at[first_point].add(toward_left)
        totals = totals.at[second_point].add(toward_right)
        return totals
    zeros_init = jnp.zeros(orbitals.shape, jnp.float32)
    return lax.fori_loop(0, PAIRS, accumulate, zeros_init)
```

```python
import functools
import math

import jax
import jax.numpy as jnp
import numpy as np
from jax import lax
from jax.experimental import pallas as pl
from jax.experimental.pallas import tpu as pltpu
from jax.sharding import PartitionSpec as P

N = 128
CHUNKS = 32
NG = 1024
ROWS = 256
MESH = pl.DeviceIdType.MESH
F32 = jnp.float32
BF16 = jnp.bfloat16

_W = np.arange(1.0, 5.0)
_COEF = np.linalg.solve(
    np.stack([_W, _W**3, _W**5, _W**7], axis=1), math.sqrt(2.0) * np.sin(np.pi * _W / 8)
)
_COEF = [float(c) for c in _COEF]


def wrap(value, size):
    return jnp.where(value >= size, value - size, value)


def root2_cos(phase):
    phase = jnp.bitwise_and(phase, 15)
    w = (4 - jnp.minimum(phase, 16 - phase)).astype(F32)
    s = w * w
    return w * (_COEF[0] + s * (_COEF[1] + s * (_COEF[2] + s * _COEF[3])))


def remote(src, dst, send_sem, recv_sem, chip, core):
    return pltpu.make_async_remote_copy(
        src_ref=src,
        dst_ref=dst,
        send_sem=send_sem,
        recv_sem=recv_sem,
        device_id=(chip, core),
        device_id_type=MESH,
    )


def build_table(gmap_ref, table):
    lane = lax.broadcasted_iota(jnp.int32, (16, 128), 1)
    scale = math.sqrt(0.5)

    @pl.loop(0, NG // 128)
    def _(block):
        row = gmap_ref[pl.ds(block, 1), :].astype(F32)
        column = jnp.transpose(jnp.broadcast_to(row, (128, 128))).astype(jnp.int32)
        for sub in range(8):
            freq = column[sub * 16 : (sub + 1) * 16, :]
            freq_x = lax.shift_right_logical(freq, 8)
            freq_y = jnp.bitwise_and(lax.shift_right_logical(freq, 4), 15)
            freq_z = jnp.bitwise_and(freq, 15)
            cos1 = root2_cos(freq_x) * scale
            sin1 = root2_cos(freq_x - 4) * scale
            cos4 = root2_cos(freq_x * 4) * scale
            sin4 = root2_cos(freq_x * 4 - 4) * scale
            cos8 = (1 - 2 * jnp.bitwise_and(freq_x, 1)).astype(F32)
            rows = pl.ds(pl.multiple_of(block * 128 + sub * 16, 16), 16)
            for half in range(2):
                coord_y = half * 8 + lax.shift_right_logical(lane, 4)
                coord_z = jnp.bitwise_and(lane, 15)
                phase = freq_y * coord_y + freq_z * coord_z
                plus = root2_cos(phase - 2)
                minus = root2_cos(phase + 2)
                for x in range(4):
                    if x:
                        plus, minus = (
                            cos1 * plus + sin1 * minus,
                            cos1 * minus - sin1 * plus,
                        )
                    later = cos4 * plus + sin4 * minus
                    for step, value in (
                        (0, plus),
                        (8, cos8 * plus),
                        (4, later),
                        (12, cos8 * later),
                    ):
                        start = (x + step) * 256 + half * 128
                        table[rows, start : start + 128] = value.astype(BF16)


def compute(screen, slot, table, blocks, density, spectrum, screened, fields):
    def side(q, s):
        low = blocks[4 * q + s].astype(F32)
        high = blocks[4 * q + 2 + s].astype(F32)
        return jnp.concatenate([low, high], axis=0)

    @pl.loop(0, CHUNKS)
    def _(q):
        left, right = side(q, 0), side(q, 1)
        product = left[:, None, :] * right[None, :, :]
        lanes = pl.ds(pl.multiple_of(q * 128, 128), 128)
        density[:, lanes] = product.reshape(ROWS, 128).astype(BF16)

    @pl.loop(0, NG // 256)
    def _(t):
        rows = pl.ds(pl.multiple_of(t * 256, 256), 256)
        value = lax.dot_general(
            density[...], table[rows, :], (((1,), (1,)), ((), ())), preferred_element_type=F32
        )
        spectrum[:, rows] = (value * (1.0 / 64.0)).astype(BF16)

    @pl.loop(0, NG // 256)
    def _(t):
        columns = pl.ds(pl.multiple_of(t * 256, 256), 256)
        value = jnp.dot(spectrum[...], screen[slot, :, columns], preferred_element_type=F32)
        screened[:, columns] = (value * (1.0 / 64.0)).astype(BF16)

    @pl.loop(0, CHUNKS // 2)
    def _(t):
        lanes = pl.ds(pl.multiple_of(t * 256, 256), 256)
        value = jnp.dot(screened[...], table[:, lanes], preferred_element_type=F32)
        for h in range(2):
            q = 2 * t + h
            left, right = side(q, 0), side(q, 1)
            potential = value[:, h * 128 : (h + 1) * 128].reshape(16, 16, 128)
            first = jnp.sum(potential * right[None, :, :], axis=1).astype(BF16)
            second = jnp.sum(potential * left[:, None, :], axis=0).astype(BF16)
            fields[4 * q + 0] = first[0:8]
            fields[4 * q + 1] = second[0:8]
            fields[4 * q + 2] = first[8:16]
            fields[4 * q + 3] = second[8:16]


def kernel(
    pair_ref, q_ref, gmap_ref, x_ref, screening_ref, o_ref,
    gathered, outgoing, blocks, fields, returned, resorted, arrived,
    table, screen, density, spectrum, screened,
    send_sem, recv_sem, local_sem, entry_sem,
):
    me = lax.axis_index("kq")
    core = lax.axis_index("band")
    chunk = lax.div(me, 4)
    plane = lax.div(lax.rem(me, 4), 2)
    slot = lax.rem(me, 2)
    same = plane == core

    load = pltpu.make_async_copy(screening_ref, screen, local_sem.at[4])
    load.start()

    at_x, at_y, at_z = lax.div(me, 32), lax.rem(lax.div(me, 8), 4), lax.rem(me, 8)
    along_z = [at_x * 32 + at_y * 8 + lax.rem(at_z + i, 8) for i in (4, 3, 5, 2, 6, 1, 7)]
    along_y = [at_x * 32 + lax.rem(at_y + i, 4) * 8 + at_z for i in (2, 1, 3)]
    along_x = [lax.rem(at_x + i, 4) * 32 + at_y * 8 + at_z for i in (2, 1, 3)]
    barrier = pltpu.get_barrier_semaphore()

    def greet(sem, chip, to_core):
        pl.semaphore_signal(sem, inc=1, device_id=(chip, to_core), device_id_type=MESH)

    for chip in along_z + along_y + along_x:
        greet(barrier, chip, core)
    greet(barrier, me, 1 - core)
    pl.semaphore_wait(barrier, 14)
    for chip in along_y:
        greet(entry_sem.at[0], chip, core)
    pl.semaphore_wait(entry_sem.at[0], 3)
    for chip in along_x:
        greet(entry_sem.at[1], chip, core)
    pl.semaphore_wait(entry_sem.at[1], 3)
    greet(entry_sem.at[2], me, 1 - core)
    pl.semaphore_wait(entry_sem.at[2], 1)

    @pl.loop(0, CHUNKS)
    def _(i):
        q = wrap(chunk + i, CHUNKS)
        piece = x_ref.at[:, pl.ds(pl.multiple_of(q * 128, 128), 128)]
        for s in range(2):
            chip = 4 * q + 2 * core + s
            for c in range(2):
                here = jnp.logical_and(chip == me, c == core)

                @pl.when(here)
                def _():
                    pltpu.make_async_copy(piece, gathered.at[me], local_sem.at[0]).start()

                @pl.when(jnp.logical_not(here))
                def _():
                    remote(
                        piece, gathered.at[me], send_sem.at[0], recv_sem.at[0], chip, c
                    ).start()

    build_table(gmap_ref, table)

    def finish(phase, src, dst, local, count):
        if local is not None:
            pltpu.make_async_copy(src.at[me], dst.at[me], local_sem.at[phase]).wait()
        both = remote(
            src.at[pl.ds(0, count)], dst.at[pl.ds(0, count)],
            send_sem.at[phase], recv_sem.at[phase], me, core,
        )
        both.wait_send()
        both.wait_recv()

    @pl.when(same)
    def _():
        finish(0, gathered, gathered, True, N - 1)

    @pl.when(jnp.logical_not(same))
    def _():
        finish(0, gathered, gathered, None, N)

    shift = pair_ref[core, slot]

    @pl.loop(0, N, unroll=8)
    def _(o):
        outgoing[o] = gathered[wrap(o + shift, N)]

    def exchange(phase, src, dst):
        @pl.loop(1, N)
        def _(i):
            o = wrap(me + i, N)
            remote(src.at[o], dst.at[me], send_sem.at[phase], recv_sem.at[phase], o, core).start()

        pltpu.make_async_copy(src.at[me], dst.at[me], local_sem.at[phase]).start()

    exchange(1, outgoing, blocks)
    load.wait()
    finish(1, outgoing, blocks, True, N - 1)

    compute(screen, lax.rem(q_ref[core], 2), table, blocks, density, spectrum, screened, fields)

    exchange(2, fields, returned)
    finish(2, fields, returned, True, N - 1)

    @pl.loop(0, N, unroll=8)
    def _(k):
        resorted[k] = returned[wrap(k + N - shift, N)]

    place = 4 * chunk + 2 * slot + core

    @pl.loop(1, N)
    def _(i):
        k = wrap(me + i, N)
        remote(
            resorted.at[k], arrived.at[place], send_sem.at[3], recv_sem.at[3], k, plane
        ).start()

    def close(count):
        both = remote(
            resorted.at[pl.ds(0, count)], arrived.at[pl.ds(0, count)],
            send_sem.at[3], recv_sem.at[3], me, core,
        )
        both.wait_send()
        both.wait_recv()

    @pl.when(same)
    def _():
        own = pltpu.make_async_copy(resorted.at[me], arrived.at[place], local_sem.at[3])
        own.start()
        own.wait()
        close(N - 1)

    @pl.when(jnp.logical_not(same))
    def _():
        remote(
            resorted.at[me], arrived.at[place], send_sem.at[3], recv_sem.at[3], me, plane
        ).start()
        close(N)

    for q in range(CHUNKS):
        terms = [arrived[4 * q + j].astype(F32) for j in range(4)]
        o_ref[:, q * 128 : (q + 1) * 128] = (terms[0] + terms[1]) + (terms[2] + terms[3])


def shards(orbitals, screening, pair_k, pair_q, gmap):
    vmem = pl.BlockSpec(memory_space=pltpu.VMEM)
    smem = pl.BlockSpec(memory_space=pltpu.SMEM)
    piece = pltpu.VMEM((N, 8, 128), BF16)
    dma = pltpu.SemaphoreType.DMA
    field = pl.pallas_call(
        kernel,
        out_shape=jax.ShapeDtypeStruct((8, 4096), F32),
        in_specs=[smem, smem, vmem, vmem, pl.BlockSpec(memory_space=pl.ANY)],
        out_specs=vmem,
        scratch_shapes=[piece] * 7
        + [
            pltpu.VMEM((NG, 4096), BF16),
            pltpu.VMEM((2, NG, NG), BF16),
            pltpu.VMEM((ROWS, 4096), BF16),
            pltpu.VMEM((ROWS, NG), BF16),
            pltpu.VMEM((ROWS, NG), BF16),
            dma((4,)),
            dma((4,)),
            dma((5,)),
            pltpu.SemaphoreType.REGULAR((3,)),
        ],
        compiler_params=pltpu.CompilerParams(
            collective_id=0, has_side_effects=True, vmem_limit_bytes=48 << 20
        ),
    )(pair_k[:2], pair_q, gmap.reshape(8, 128), orbitals[0], screening)
    return field[None]


def solution(mesh):
    in_specs = (P("kq", "band", None), P("kq", None, None), P(), P("kq"), P())
    out_specs = P("kq", "band", None)
    return jax.shard_map(shards, mesh=mesh, in_specs=in_specs, out_specs=out_specs, check_vma=False)
```

```python
import functools
import math

import jax
import jax.numpy as jnp
import numpy as np
from jax import lax
from jax.experimental import pallas as pl
from jax.experimental.pallas import tpu as pltpu
from jax.sharding import PartitionSpec as P

N = 128
CHUNKS = 32
NG = 1024
ROWS = 256
MESH = pl.DeviceIdType.MESH
F32 = jnp.float32
BF16 = jnp.bfloat16

_W = np.arange(1.0, 5.0)
_COEF = np.linalg.solve(
    np.stack([_W, _W**3, _W**5, _W**7], axis=1), math.sqrt(2.0) * np.sin(np.pi * _W / 8)
)
_COEF = [float(c) for c in _COEF]


def wrap(value, size):
    return jnp.where(value >= size, value - size, value)


def root2_cos(phase):
    phase = jnp.bitwise_and(phase, 15)
    w = (4 - jnp.minimum(phase, 16 - phase)).astype(F32)
    s = w * w
    return w * (_COEF[0] + s * (_COEF[1] + s * (_COEF[2] + s * _COEF[3])))


def remote(src, dst, send_sem, recv_sem, chip, core):
    return pltpu.make_async_remote_copy(
        src_ref=src,
        dst_ref=dst,
        send_sem=send_sem,
        recv_sem=recv_sem,
        device_id=(chip, core),
        device_id_type=MESH,
    )


def build_table(gmap_ref, table):
    lane = lax.broadcasted_iota(jnp.int32, (16, 128), 1)
    scale = math.sqrt(0.5)

    @pl.loop(0, NG // 128)
    def _(block):
        row = gmap_ref[pl.ds(block, 1), :].astype(F32)
        column = jnp.transpose(jnp.broadcast_to(row, (128, 128))).astype(jnp.int32)
        for sub in range(8):
            freq = column[sub * 16 : (sub + 1) * 16, :]
            freq_x = lax.shift_right_logical(freq, 8)
            freq_y = jnp.bitwise_and(lax.shift_right_logical(freq, 4), 15)
            freq_z = jnp.bitwise_and(freq, 15)
            cos1 = root2_cos(freq_x) * scale
            sin1 = root2_cos(freq_x - 4) * scale
            cos4 = root2_cos(freq_x * 4) * scale
            sin4 = root2_cos(freq_x * 4 - 4) * scale
            cos8 = (1 - 2 * jnp.bitwise_and(freq_x, 1)).astype(F32)
            rows = pl.ds(pl.multiple_of(block * 128 + sub * 16, 16), 16)
            for half in range(2):
                coord_y = half * 8 + lax.shift_right_logical(lane, 4)
                coord_z = jnp.bitwise_and(lane, 15)
                phase = freq_y * coord_y + freq_z * coord_z
                plus = root2_cos(phase - 2)
                minus = root2_cos(phase + 2)
                for x in range(4):
                    if x:
                        plus, minus = (
                            cos1 * plus + sin1 * minus,
                            cos1 * minus - sin1 * plus,
                        )
                    later = cos4 * plus + sin4 * minus
                    for step, value in (
                        (0, plus),
                        (8, cos8 * plus),
                        (4, later),
                        (12, cos8 * later),
                    ):
                        start = (x + step) * 256 + half * 128
                        table[rows, start : start + 128] = value.astype(BF16)


def side(blocks, q, s):
    return jnp.concatenate([blocks[4 * q + b, s].astype(F32) for b in range(4)], axis=0)


def stage_density(blocks, density):
    @pl.loop(0, CHUNKS)
    def _(q):
        left, right = side(blocks, q, 0), side(blocks, q, 1)
        product = left[:, None, :] * right[None, :, :]
        lanes = pl.ds(pl.multiple_of(q * 128, 128), 128)
        density[:, lanes] = product.reshape(ROWS, 128).astype(BF16)


def stage_one(density, table, spectrum):
    value = lax.dot_general(
        density[...], table[...], (((1,), (1,)), ((), ())), preferred_element_type=F32
    )
    spectrum[...] = (value * (1.0 / 64.0)).astype(BF16)


def stage_two(spectrum, screen, slot, screened):
    value = jnp.dot(spectrum[...], screen[slot], preferred_element_type=F32)
    screened[...] = (value * (1.0 / 64.0)).astype(BF16)


def stage_three(screened, table, blocks, fields):
    value = jnp.dot(screened[...], table[...], preferred_element_type=F32)
    for q in range(CHUNKS):
        left, right = side(blocks, q, 0), side(blocks, q, 1)
        potential = value[:, q * 128 : (q + 1) * 128].reshape(16, 16, 128)
        first = jnp.sum(potential * right[None, :, :], axis=1)
        second = jnp.sum(potential * left[:, None, :], axis=0)
        for b in range(4):
            fields[4 * q + b, 0] = first[4 * b : 4 * b + 4].astype(BF16)
            fields[4 * q + b, 1] = second[4 * b : 4 * b + 4].astype(BF16)


def compute(screen, slot, table, blocks, density, spectrum, screened, fields):
    stage_density(blocks, density)
    stage_one(density, table, spectrum)
    stage_two(spectrum, screen, slot, screened)
    stage_three(screened, table, blocks, fields)


def kernel(
    pair_ref, q_ref, gmap_ref, x_ref, screening_ref, o_ref,
    pieces, gathered, outgoing, blocks, fields, returned, resorted, arrived,
    table, screen, density, spectrum, screened,
    send_sem, recv_sem, local_sem, entry_sem,
):
    me = lax.axis_index("kq")
    core = lax.axis_index("band")
    chunk = lax.div(me, 4)
    plane = lax.div(lax.rem(me, 4), 2)
    same = plane == core

    load = pltpu.make_async_copy(screening_ref, screen, local_sem.at[4])
    load.start()

    for q in range(CHUNKS):
        block = x_ref[:, q * 128 : (q + 1) * 128].astype(F32)
        for h in range(2):
            pieces[q, h] = block[4 * h : 4 * h + 4].astype(BF16)

    at_x, at_y, at_z = lax.div(me, 32), lax.rem(lax.div(me, 8), 4), lax.rem(me, 8)
    along_z = [at_x * 32 + at_y * 8 + lax.rem(at_z + i, 8) for i in (4, 3, 5, 2, 6, 1, 7)]
    along_y = [at_x * 32 + lax.rem(at_y + i, 4) * 8 + at_z for i in (2, 1, 3)]
    along_x = [lax.rem(at_x + i, 4) * 32 + at_y * 8 + at_z for i in (2, 1, 3)]
    barrier = pltpu.get_barrier_semaphore()

    def greet(sem, chip, to_core):
        pl.semaphore_signal(sem, inc=1, device_id=(chip, to_core), device_id_type=MESH)

    for chip in along_z + along_y + along_x:
        greet(barrier, chip, core)
    greet(barrier, me, 1 - core)
    pl.semaphore_wait(barrier, 14)
    for chip in along_y:
        greet(entry_sem.at[0], chip, core)
    pl.semaphore_wait(entry_sem.at[0], 3)
    for chip in along_x:
        greet(entry_sem.at[1], chip, core)
    pl.semaphore_wait(entry_sem.at[1], 3)
    greet(entry_sem.at[2], me, 1 - core)
    pl.semaphore_wait(entry_sem.at[2], 1)

    def far_first(send):
        for dz in (4, 3, 5, 2, 6, 1, 7):
            z = lax.rem(at_z + dz, 8)

            @pl.loop(0, 16)
            def _(i):
                x = lax.rem(at_x + 2 + lax.div(i, 4), 4)
                y = lax.rem(at_y + 2 + lax.rem(i, 4), 4)
                send(x * 32 + y * 8 + z)

        @pl.loop(1, 16)
        def _(i):
            x = lax.rem(at_x + lax.div(i, 4), 4)
            y = lax.rem(at_y + lax.rem(i, 4), 4)
            send(x * 32 + y * 8 + at_z)

    for e in (1, 0):
        z_high = lax.rem(lax.div(at_z, 4) + e, 2)

        @pl.loop(0, 16)
        def _(i):
            x = lax.rem(at_x + 2 + lax.div(i, 4), 4)
            y = lax.rem(at_y + 2 + lax.rem(i, 4), 4)
            q = x * 8 + y * 2 + z_high
            for h in range(2):
                chip = 4 * q + 2 * core + h
                for c in range(2):
                    here = jnp.logical_and(chip == me, c == core)

                    @pl.when(here)
                    def _():
                        pltpu.make_async_copy(
                            pieces.at[q, h], gathered.at[me], local_sem.at[0]
                        ).start()

                    @pl.when(jnp.logical_not(here))
                    def _():
                        remote(
                            pieces.at[q, h], gathered.at[me],
                            send_sem.at[0], recv_sem.at[0], chip, c,
                        ).start()

    build_table(gmap_ref, table)

    def finish(phase, src, dst, local, count):
        if local:
            pltpu.make_async_copy(src.at[me], dst.at[me], local_sem.at[phase]).wait()
        both = remote(
            src.at[pl.ds(0, count)], dst.at[pl.ds(0, count)],
            send_sem.at[phase], recv_sem.at[phase], me, core,
        )
        both.wait_send()
        both.wait_recv()

    @pl.when(same)
    def _():
        finish(0, gathered, gathered, True, N - 1)

    @pl.when(jnp.logical_not(same))
    def _():
        finish(0, gathered, gathered, False, N)

    shifts = [pair_ref[core, s] for s in range(2)]

    @pl.loop(0, N, unroll=8)
    def _(o):
        for s in range(2):
            outgoing[o, s] = gathered[wrap(o + shifts[s], N)]

    def exchange(phase, src, dst):
        def send(chip):
            remote(
                src.at[chip], dst.at[me], send_sem.at[phase], recv_sem.at[phase], chip, core
            ).start()

        far_first(send)
        pltpu.make_async_copy(src.at[me], dst.at[me], local_sem.at[phase]).start()

    exchange(1, outgoing, blocks)
    load.wait()
    finish(1, outgoing, blocks, True, N - 1)

    compute(screen, lax.rem(q_ref[core], 2), table, blocks, density, spectrum, screened, fields)

    exchange(2, fields, returned)
    finish(2, fields, returned, True, N - 1)

    @pl.loop(0, N, unroll=8)
    def _(k):
        first = returned[wrap(k + N - shifts[0], N), 0].astype(F32)
        second = returned[wrap(k + N - shifts[1], N), 1].astype(F32)
        resorted[k] = (first + second).astype(BF16)

    place = 4 * chunk + 2 * lax.rem(me, 2) + core

    def deliver(chip):
        remote(
            resorted.at[chip], arrived.at[place], send_sem.at[3], recv_sem.at[3], chip, plane
        ).start()

    far_first(deliver)

    def close(count):
        both = remote(
            resorted.at[pl.ds(0, count)], arrived.at[pl.ds(0, count)],
            send_sem.at[3], recv_sem.at[3], me, core,
        )
        both.wait_send()
        both.wait_recv()

    @pl.when(same)
    def _():
        own = pltpu.make_async_copy(resorted.at[me], arrived.at[place], local_sem.at[3])
        own.start()
        own.wait()
        close(N - 1)

    @pl.when(jnp.logical_not(same))
    def _():
        deliver(me)
        close(N)

    for q in range(CHUNKS):
        for h in range(2):
            terms = [arrived[4 * q + 2 * h + i].astype(F32) for i in range(2)]
            o_ref[4 * h : 4 * h + 4, q * 128 : (q + 1) * 128] = terms[0] + terms[1]


def shards(orbitals, screening, pair_k, pair_q, gmap):
    vmem = pl.BlockSpec(memory_space=pltpu.VMEM)
    smem = pl.BlockSpec(memory_space=pltpu.SMEM)
    single = pltpu.VMEM((N, 4, 128), BF16)
    double = pltpu.VMEM((N, 2, 4, 128), BF16)
    dma = pltpu.SemaphoreType.DMA
    field = pl.pallas_call(
        kernel,
        out_shape=jax.ShapeDtypeStruct((8, 4096), F32),
        in_specs=[smem, smem, vmem, vmem, pl.BlockSpec(memory_space=pl.ANY)],
        out_specs=vmem,
        scratch_shapes=[pltpu.VMEM((CHUNKS, 2, 4, 128), BF16), single]
        + [double] * 4
        + [single] * 2
        + [
            pltpu.VMEM((NG, 4096), BF16),
            pltpu.VMEM((2, NG, NG), BF16),
            pltpu.VMEM((ROWS, 4096), BF16),
            pltpu.VMEM((ROWS, NG), BF16),
            pltpu.VMEM((ROWS, NG), BF16),
            dma((4,)),
            dma((4,)),
            dma((5,)),
            pltpu.SemaphoreType.REGULAR((3,)),
        ],
        compiler_params=pltpu.CompilerParams(
            collective_id=0, has_side_effects=True, vmem_limit_bytes=48 << 20
        ),
    )(pair_k[:2], pair_q, gmap.reshape(8, 128), orbitals[0], screening)
    return field[None]


def solution(mesh):
    in_specs = (P("kq", "band", None), P("kq", None, None), P(), P("kq"), P())
    out_specs = P("kq", "band", None)
    return jax.shard_map(shards, mesh=mesh, in_specs=in_specs, out_specs=out_specs, check_vma=False)
```

```python
import functools
import math

import jax
import jax.numpy as jnp
import numpy as np
from jax import lax
from jax.experimental import pallas as pl
from jax.experimental.pallas import tpu as pltpu
from jax.sharding import PartitionSpec as P

N = 128
CHUNKS = 32
NG = 1024
ROWS = 256
MESH = pl.DeviceIdType.MESH
F32 = jnp.float32
BF16 = jnp.bfloat16

_W = np.arange(1.0, 5.0)
_COEF = np.linalg.solve(
    np.stack([_W, _W**3, _W**5, _W**7], axis=1), math.sqrt(2.0) * np.sin(np.pi * _W / 8)
)
_COEF = [float(c) for c in _COEF]


def wrap(value, size):
    return jnp.where(value >= size, value - size, value)


def root2_cos(phase):
    phase = jnp.bitwise_and(phase, 15)
    w = (4 - jnp.minimum(phase, 16 - phase)).astype(F32)
    s = w * w
    return w * (_COEF[0] + s * (_COEF[1] + s * (_COEF[2] + s * _COEF[3])))


def remote(src, dst, send_sem, recv_sem, chip, core):
    return pltpu.make_async_remote_copy(
        src_ref=src,
        dst_ref=dst,
        send_sem=send_sem,
        recv_sem=recv_sem,
        device_id=(chip, core),
        device_id_type=MESH,
    )


def build_table(gmap_ref, table):
    lane = lax.broadcasted_iota(jnp.int32, (16, 128), 1)
    scale = math.sqrt(0.5)

    @pl.loop(0, NG // 128)
    def _(block):
        row = gmap_ref[pl.ds(block, 1), :].astype(F32)
        column = jnp.transpose(jnp.broadcast_to(row, (128, 128))).astype(jnp.int32)
        for sub in range(8):
            freq = column[sub * 16 : (sub + 1) * 16, :]
            freq_x = lax.shift_right_logical(freq, 8)
            freq_y = jnp.bitwise_and(lax.shift_right_logical(freq, 4), 15)
            freq_z = jnp.bitwise_and(freq, 15)
            cos1 = root2_cos(freq_x) * scale
            sin1 = root2_cos(freq_x - 4) * scale
            cos4 = root2_cos(freq_x * 4) * scale
            sin4 = root2_cos(freq_x * 4 - 4) * scale
            cos8 = (1 - 2 * jnp.bitwise_and(freq_x, 1)).astype(F32)
            rows = pl.ds(pl.multiple_of(block * 128 + sub * 16, 16), 16)
            for half in range(2):
                coord_y = half * 8 + lax.shift_right_logical(lane, 4)
                coord_z = jnp.bitwise_and(lane, 15)
                phase = freq_y * coord_y + freq_z * coord_z
                plus = root2_cos(phase - 2)
                minus = root2_cos(phase + 2)
                for x in range(4):
                    if x:
                        plus, minus = (
                            cos1 * plus + sin1 * minus,
                            cos1 * minus - sin1 * plus,
                        )
                    later = cos4 * plus + sin4 * minus
                    for step, value in (
                        (0, plus),
                        (8, cos8 * plus),
                        (4, later),
                        (12, cos8 * later),
                    ):
                        start = (x + step) * 256 + half * 128
                        table[rows, start : start + 128] = value.astype(BF16)


def side(blocks, q, s):
    return jnp.concatenate([blocks[4 * q + b, s].astype(F32) for b in range(4)], axis=0)


def stage_density(blocks, density):
    @pl.loop(0, CHUNKS)
    def _(q):
        left, right = side(blocks, q, 0), side(blocks, q, 1)
        product = left[:, None, :] * right[None, :, :]
        lanes = pl.ds(pl.multiple_of(q * 128, 128), 128)
        density[:, lanes] = product.reshape(ROWS, 128).astype(BF16)


def stage_one(density, table, spectrum):
    value = lax.dot_general(
        density[...], table[...], (((1,), (1,)), ((), ())), preferred_element_type=F32
    )
    spectrum[...] = (value * (1.0 / 64.0)).astype(BF16)


def stage_two(spectrum, screen, slot, screened):
    value = jnp.dot(spectrum[...], screen[slot], preferred_element_type=F32)
    screened[...] = (value * (1.0 / 64.0)).astype(BF16)


def stage_three(screened, table, blocks, fields):
    value = jnp.dot(screened[...], table[...], preferred_element_type=F32)
    for q in range(CHUNKS):
        left, right = side(blocks, q, 0), side(blocks, q, 1)
        potential = value[:, q * 128 : (q + 1) * 128].reshape(16, 16, 128)
        first = jnp.sum(potential * right[None, :, :], axis=1)
        second = jnp.sum(potential * left[:, None, :], axis=0)
        for b in range(4):
            fields[4 * q + b, 0] = first[4 * b : 4 * b + 4].astype(BF16)
            fields[4 * q + b, 1] = second[4 * b : 4 * b + 4].astype(BF16)


def compute(screen, slot, table, blocks, density, spectrum, screened, fields):
    stage_density(blocks, density)
    stage_one(density, table, spectrum)
    stage_two(spectrum, screen, slot, screened)
    stage_three(screened, table, blocks, fields)


def kernel(
    pair_hbm, q_hbm, gmap_hbm, x_hbm, screening_ref, o_ref,
    pair_ref, q_ref, gmap_ref, x_ref, pieces, gathered, outgoing, blocks, fields, returned, resorted, arrived,
    table, screen, density, spectrum, screened,
    send_sem, recv_sem, local_sem, entry_sem, load_sem,
):
    me = lax.axis_index("kq")
    core = lax.axis_index("band")
    chunk = lax.div(me, 4)
    plane = lax.div(lax.rem(me, 4), 2)
    same = plane == core

    at_x, at_y, at_z = lax.div(me, 32), lax.rem(lax.div(me, 8), 4), lax.rem(me, 8)
    along_z = [at_x * 32 + at_y * 8 + lax.rem(at_z + i, 8) for i in (4, 3, 5, 2, 6, 1, 7)]
    along_y = [at_x * 32 + lax.rem(at_y + i, 4) * 8 + at_z for i in (2, 1, 3)]
    along_x = [lax.rem(at_x + i, 4) * 32 + at_y * 8 + at_z for i in (2, 1, 3)]
    barrier = pltpu.get_barrier_semaphore()

    def greet(sem, chip, to_core):
        pl.semaphore_signal(sem, inc=1, device_id=(chip, to_core), device_id_type=MESH)

    for chip in along_z + along_y + along_x:
        greet(barrier, chip, core)
    greet(barrier, me, 1 - core)

    loads = [
        pltpu.make_async_copy(src, dst, load_sem.at[i])
        for i, (src, dst) in enumerate(
            (
                (x_hbm.at[0], x_ref),
                (gmap_hbm, gmap_ref),
                (pair_hbm, pair_ref),
                (q_hbm, q_ref),
            )
        )
    ]
    load = pltpu.make_async_copy(screening_ref, screen, local_sem.at[4])
    for copy in loads:
        copy.start()
    load.start()
    loads[0].wait()
    for q in range(CHUNKS):
        block = x_ref[:, q * 128 : (q + 1) * 128].astype(F32)
        for h in range(2):
            pieces[q, h] = block[4 * h : 4 * h + 4].astype(BF16)
    for copy in loads[1:]:
        copy.wait()

    pl.semaphore_wait(barrier, 14)
    for chip in along_y:
        greet(entry_sem.at[0], chip, core)
    pl.semaphore_wait(entry_sem.at[0], 3)
    for chip in along_x:
        greet(entry_sem.at[1], chip, core)
    pl.semaphore_wait(entry_sem.at[1], 3)
    greet(entry_sem.at[2], me, 1 - core)
    pl.semaphore_wait(entry_sem.at[2], 1)

    columns = [
        lax.rem(at_x + 2 + i // 4, 4) * 32 + lax.rem(at_y + 2 + i % 4, 4) * 8
        for i in range(16)
    ]

    def far_first(send):
        @pl.loop(0, 7)
        def _(i):
            half = lax.div(i + 1, 2)
            z = lax.rem(at_z + 4 + (1 - 2 * lax.rem(i, 2)) * half, 8)
            for column in columns:
                send(column + z)

        for i in range(16):
            if i != 10:
                send(columns[i] + at_z)

    def scatter(q, h, chip, c):
        remote(
            pieces.at[q, h], gathered.at[me], send_sem.at[0], recv_sem.at[0], chip, c
        ).start()

    for e in (1, 0):
        z_high = lax.rem(lax.div(at_z, 4) + e, 2)
        for i in range(16):
            chip0 = columns[i] + 4 * z_high + 2 * core
            q = lax.div(chip0, 4)
            for h in range(2):
                if e == 1 or i != 10:
                    scatter(q, h, chip0 + h, 0)
                    scatter(q, h, chip0 + h, 1)
                    continue
                away = chip0 + h != me

                @pl.when(away)
                def _():
                    scatter(q, h, chip0 + h, 0)
                    scatter(q, h, chip0 + h, 1)

                @pl.when(jnp.logical_not(away))
                def _():
                    scatter(q, h, me, 1 - core)
                    pltpu.make_async_copy(
                        pieces.at[q, h], gathered.at[me], local_sem.at[0]
                    ).start()

    build_table(gmap_ref, table)

    def finish(phase, src, dst, local, count):
        if local:
            pltpu.make_async_copy(src.at[me], dst.at[me], local_sem.at[phase]).wait()
        both = remote(
            src.at[pl.ds(0, count)], dst.at[pl.ds(0, count)],
            send_sem.at[phase], recv_sem.at[phase], me, core,
        )
        both.wait_send()
        both.wait_recv()

    @pl.when(same)
    def _():
        finish(0, gathered, gathered, True, N - 1)

    @pl.when(jnp.logical_not(same))
    def _():
        finish(0, gathered, gathered, False, N)

    shifts = [pair_ref[s, core] for s in range(2)]

    @pl.loop(0, N, unroll=8)
    def _(o):
        for s in range(2):
            outgoing[o, s] = gathered[wrap(o + shifts[s], N)]

    def exchange(phase, src, dst):
        def send(chip):
            remote(
                src.at[chip], dst.at[me], send_sem.at[phase], recv_sem.at[phase], chip, core
            ).start()

        far_first(send)
        pltpu.make_async_copy(src.at[me], dst.at[me], local_sem.at[phase]).start()

    exchange(1, outgoing, blocks)
    load.wait()
    finish(1, outgoing, blocks, True, N - 1)

    compute(screen, lax.rem(q_ref[core], 2), table, blocks, density, spectrum, screened, fields)

    exchange(2, fields, returned)
    finish(2, fields, returned, True, N - 1)

    @pl.loop(0, N, unroll=8)
    def _(k):
        first = returned[wrap(k + N - shifts[0], N), 0].astype(F32)
        second = returned[wrap(k + N - shifts[1], N), 1].astype(F32)
        resorted[k] = (first + second).astype(BF16)

    place = 4 * chunk + 2 * lax.rem(me, 2) + core

    def deliver(chip):
        remote(
            resorted.at[chip], arrived.at[place], send_sem.at[3], recv_sem.at[3], chip, plane
        ).start()

    far_first(deliver)

    def close(count):
        both = remote(
            resorted.at[pl.ds(0, count)], arrived.at[pl.ds(0, count)],
            send_sem.at[3], recv_sem.at[3], me, core,
        )
        both.wait_send()
        both.wait_recv()

    @pl.when(same)
    def _():
        own = pltpu.make_async_copy(resorted.at[me], arrived.at[place], local_sem.at[3])
        own.start()
        own.wait()
        close(N - 1)

    @pl.when(jnp.logical_not(same))
    def _():
        deliver(me)
        close(N)

    for q in range(CHUNKS):
        for h in range(2):
            terms = [arrived[4 * q + 2 * h + i].astype(F32) for i in range(2)]
            o_ref[4 * h : 4 * h + 4, q * 128 : (q + 1) * 128] = terms[0] + terms[1]


def shards(orbitals, screening, pair_k, pair_q, gmap):
    vmem = pl.BlockSpec(memory_space=pltpu.VMEM)
    single = pltpu.VMEM((N, 4, 128), BF16)
    double = pltpu.VMEM((N, 2, 4, 128), BF16)
    dma = pltpu.SemaphoreType.DMA
    field = pl.pallas_call(
        kernel,
        out_shape=jax.ShapeDtypeStruct((8, 4096), F32),
        in_specs=[pl.BlockSpec(memory_space=pltpu.HBM)] * 5,
        out_specs=vmem,
        scratch_shapes=[
            pltpu.SMEM((2, 256), jnp.int32),
            pltpu.SMEM((2,), jnp.int32),
            pltpu.VMEM((8, 128), jnp.int32),
            pltpu.VMEM((8, 4096), BF16),
            pltpu.VMEM((CHUNKS, 2, 4, 128), BF16),
            single,
        ]
        + [double] * 4
        + [single] * 2
        + [
            pltpu.VMEM((NG, 4096), BF16),
            pltpu.VMEM((2, NG, NG), BF16),
            pltpu.VMEM((ROWS, 4096), BF16),
            pltpu.VMEM((ROWS, NG), BF16),
            pltpu.VMEM((ROWS, NG), BF16),
            dma((4,)),
            dma((4,)),
            dma((5,)),
            pltpu.SemaphoreType.REGULAR((3,)),
            dma((4,)),
        ],
        compiler_params=pltpu.CompilerParams(
            collective_id=0, has_side_effects=True, vmem_limit_bytes=67043328
        ),
    )(pair_k.T, pair_q, gmap.reshape(8, 128), orbitals, screening)
    return field[None]


def solution(mesh):
    in_specs = (P("kq", "band", None), P("kq", None, None), P(), P("kq"), P())
    out_specs = P("kq", "band", None)
    return jax.shard_map(shards, mesh=mesh, in_specs=in_specs, out_specs=out_specs, check_vma=False)
```

```python
import functools
import math

import jax
import jax.numpy as jnp
import numpy as np
from jax import lax
from jax.experimental import pallas as pl
from jax.experimental.pallas import tpu as pltpu
from jax.sharding import PartitionSpec as P

N = 128
CHUNKS = 32
NG = 1024
ROWS = 256
MESH = pl.DeviceIdType.MESH
F32 = jnp.float32
BF16 = jnp.bfloat16

_W = np.arange(1.0, 5.0)
_COEF = np.linalg.solve(
    np.stack([_W, _W**3, _W**5, _W**7], axis=1), math.sqrt(2.0) * np.sin(np.pi * _W / 8)
)
_COEF = [float(c) for c in _COEF]


def wrap(value, size):
    return jnp.where(value >= size, value - size, value)


def root2_cos(phase):
    phase = jnp.bitwise_and(phase, 15)
    w = (4 - jnp.minimum(phase, 16 - phase)).astype(F32)
    s = w * w
    return w * (_COEF[0] + s * (_COEF[1] + s * (_COEF[2] + s * _COEF[3])))


def remote(src, dst, send_sem, recv_sem, chip, core):
    return pltpu.make_async_remote_copy(
        src_ref=src,
        dst_ref=dst,
        send_sem=send_sem,
        recv_sem=recv_sem,
        device_id=(chip, core),
        device_id_type=MESH,
    )


def build_table(gmap_ref, table):
    lane = lax.broadcasted_iota(jnp.int32, (16, 128), 1)
    scale = math.sqrt(0.5)

    @pl.loop(0, NG // 128)
    def _(block):
        row = gmap_ref[pl.ds(block, 1), :].astype(F32)
        column = jnp.transpose(jnp.broadcast_to(row, (128, 128))).astype(jnp.int32)
        for sub in range(8):
            freq = column[sub * 16 : (sub + 1) * 16, :]
            freq_x = lax.shift_right_logical(freq, 8)
            freq_y = jnp.bitwise_and(lax.shift_right_logical(freq, 4), 15)
            freq_z = jnp.bitwise_and(freq, 15)
            cos1 = root2_cos(freq_x) * scale
            sin1 = root2_cos(freq_x - 4) * scale
            cos4 = root2_cos(freq_x * 4) * scale
            sin4 = root2_cos(freq_x * 4 - 4) * scale
            cos8 = (1 - 2 * jnp.bitwise_and(freq_x, 1)).astype(F32)
            rows = pl.ds(pl.multiple_of(block * 128 + sub * 16, 16), 16)
            for half in range(2):
                coord_y = half * 8 + lax.shift_right_logical(lane, 4)
                coord_z = jnp.bitwise_and(lane, 15)
                phase = freq_y * coord_y + freq_z * coord_z
                plus = root2_cos(phase - 2)
                minus = root2_cos(phase + 2)
                for x in range(4):
                    if x:
                        plus, minus = (
                            cos1 * plus + sin1 * minus,
                            cos1 * minus - sin1 * plus,
                        )
                    later = cos4 * plus + sin4 * minus
                    for step, value in (
                        (0, plus),
                        (8, cos8 * plus),
                        (4, later),
                        (12, cos8 * later),
                    ):
                        start = (x + step) * 256 + half * 128
                        table[rows, start : start + 128] = value.astype(BF16)


def side(blocks, q, s):
    return jnp.concatenate([blocks[4 * q + b, s].astype(F32) for b in range(4)], axis=0)


def stage_density(blocks, density):
    @pl.loop(0, CHUNKS)
    def _(q):
        left, right = side(blocks, q, 0), side(blocks, q, 1)
        product = left[:, None, :] * right[None, :, :]
        lanes = pl.ds(pl.multiple_of(q * 128, 128), 128)
        density[:, lanes] = product.reshape(ROWS, 128).astype(BF16)


def stage_one(density, table, spectrum):
    value = lax.dot_general(
        density[...], table[...], (((1,), (1,)), ((), ())), preferred_element_type=F32
    )
    spectrum[...] = (value * (1.0 / 64.0)).astype(BF16)


def stage_two(spectrum, screen, slot, screened):
    value = jnp.dot(spectrum[...], screen[slot], preferred_element_type=F32)
    screened[...] = (value * (1.0 / 64.0)).astype(BF16)


def stage_three(part, screened, table, blocks, fields):
    half = CHUNKS // 2
    lanes = slice(part * half * 128, (part + 1) * half * 128)
    value = jnp.dot(screened[...], table[:, lanes], preferred_element_type=F32)
    for i in range(half):
        q = part * half + i
        left, right = side(blocks, q, 0), side(blocks, q, 1)
        potential = value[:, i * 128 : (i + 1) * 128].reshape(16, 16, 128)
        first = jnp.sum(potential * right[None, :, :], axis=1)
        second = jnp.sum(potential * left[:, None, :], axis=0)
        for b in range(4):
            fields[4 * q + b, 0] = first[4 * b : 4 * b + 4].astype(BF16)
            fields[4 * q + b, 1] = second[4 * b : 4 * b + 4].astype(BF16)


def compute(screen, slot, table, blocks, density, spectrum, screened):
    stage_density(blocks, density)
    stage_one(density, table, spectrum)
    stage_two(spectrum, screen, slot, screened)


def kernel(
    pair_hbm, q_hbm, gmap_hbm, x_hbm, screening_ref, o_ref,
    pair_ref, q_ref, gmap_ref, x_ref, pieces, gathered, outgoing, blocks, fields, returned, resorted, arrived,
    table, screen, density, spectrum, screened,
    send_sem, recv_sem, local_sem, entry_sem, load_sem,
):
    me = lax.axis_index("kq")
    core = lax.axis_index("band")
    chunk = lax.div(me, 4)
    plane = lax.div(lax.rem(me, 4), 2)
    same = plane == core

    at_x, at_y, at_z = lax.div(me, 32), lax.rem(lax.div(me, 8), 4), lax.rem(me, 8)
    along_z = [at_x * 32 + at_y * 8 + lax.rem(at_z + i, 8) for i in (4, 3, 5, 2, 6, 1, 7)]
    along_y = [at_x * 32 + lax.rem(at_y + i, 4) * 8 + at_z for i in (2, 1, 3)]
    along_x = [lax.rem(at_x + i, 4) * 32 + at_y * 8 + at_z for i in (2, 1, 3)]
    barrier = pltpu.get_barrier_semaphore()

    def greet(sem, chip, to_core):
        pl.semaphore_signal(sem, inc=1, device_id=(chip, to_core), device_id_type=MESH)

    for chip in along_z + along_y + along_x:
        greet(barrier, chip, core)
    greet(barrier, me, 1 - core)

    loads = [
        pltpu.make_async_copy(src, dst, load_sem.at[i])
        for i, (src, dst) in enumerate(
            (
                (x_hbm.at[0], x_ref),
                (gmap_hbm, gmap_ref),
                (pair_hbm, pair_ref),
                (q_hbm, q_ref),
            )
        )
    ]
    load = pltpu.make_async_copy(screening_ref, screen, local_sem.at[4])
    for copy in loads:
        copy.start()
    load.start()
    loads[0].wait()
    for q in range(CHUNKS):
        block = x_ref[:, q * 128 : (q + 1) * 128].astype(F32)
        for h in range(2):
            pieces[q, h] = block[4 * h : 4 * h + 4].astype(BF16)
    for copy in loads[1:]:
        copy.wait()

    pl.semaphore_wait(barrier, 14)
    for chip in along_y:
        greet(entry_sem.at[0], chip, core)
    pl.semaphore_wait(entry_sem.at[0], 3)
    for chip in along_x:
        greet(entry_sem.at[1], chip, core)
    pl.semaphore_wait(entry_sem.at[1], 3)
    greet(entry_sem.at[2], me, 1 - core)
    pl.semaphore_wait(entry_sem.at[2], 1)

    columns = [
        lax.rem(at_x + 2 + i // 4, 4) * 32 + lax.rem(at_y + 2 + i % 4, 4) * 8
        for i in range(16)
    ]

    def far_first(send):
        @pl.loop(0, 7)
        def _(i):
            half = lax.div(i + 1, 2)
            z = lax.rem(at_z + 4 + (1 - 2 * lax.rem(i, 2)) * half, 8)
            for column in columns:
                send(column + z)

        for i in range(16):
            if i != 10:
                send(columns[i] + at_z)

    def scatter(q, h, chip, c):
        remote(
            pieces.at[q, h], gathered.at[me], send_sem.at[0], recv_sem.at[0], chip, c
        ).start()

    for e in (1, 0):
        z_high = lax.rem(lax.div(at_z, 4) + e, 2)
        for i in range(16):
            chip0 = columns[i] + 4 * z_high + 2 * core
            q = lax.div(chip0, 4)
            for h in range(2):
                if e == 1 or i != 10:
                    scatter(q, h, chip0 + h, 0)
                    scatter(q, h, chip0 + h, 1)
                    continue
                away = chip0 + h != me

                @pl.when(away)
                def _():
                    scatter(q, h, chip0 + h, 0)
                    scatter(q, h, chip0 + h, 1)

                @pl.when(jnp.logical_not(away))
                def _():
                    scatter(q, h, me, 1 - core)
                    pltpu.make_async_copy(
                        pieces.at[q, h], gathered.at[me], local_sem.at[0]
                    ).start()

    build_table(gmap_ref, table)

    def finish(phase, src, dst, local, count):
        if local:
            pltpu.make_async_copy(src.at[me], dst.at[me], local_sem.at[phase]).wait()
        both = remote(
            src.at[pl.ds(0, count)], dst.at[pl.ds(0, count)],
            send_sem.at[phase], recv_sem.at[phase], me, core,
        )
        both.wait_recv()

    @pl.when(same)
    def _():
        finish(0, gathered, gathered, True, N - 1)

    @pl.when(jnp.logical_not(same))
    def _():
        finish(0, gathered, gathered, False, N)

    shifts = [pair_ref[s, core] for s in range(2)]

    @pl.loop(0, N, unroll=8)
    def _(o):
        for s in range(2):
            outgoing[o, s] = gathered[wrap(o + shifts[s], N)]

    def exchange(phase, src, dst):
        def send(chip):
            remote(
                src.at[chip], dst.at[me], send_sem.at[phase], recv_sem.at[phase], chip, core
            ).start()

        far_first(send)
        pltpu.make_async_copy(src.at[me], dst.at[me], local_sem.at[phase]).start()

    exchange(1, outgoing, blocks)
    load.wait()
    finish(1, outgoing, blocks, True, N - 1)

    compute(screen, lax.rem(q_ref[core], 2), table, blocks, density, spectrum, screened)

    def give(chip):
        remote(
            fields.at[chip], returned.at[me], send_sem.at[2], recv_sem.at[2], chip, core
        ).start()

    for part in range(2):
        stage_three(part, screened, table, blocks, fields)
        bases = [x * 32 + y * 8 for x in (2 * part, 2 * part + 1) for y in range(4)]

        @pl.loop(0, 7)
        def _(i):
            half = lax.div(i + 1, 2)
            z = lax.rem(at_z + 4 + (1 - 2 * lax.rem(i, 2)) * half, 8)
            for base in bases:
                give(base + z)

        for base in bases:

            @pl.when(base + at_z != me)
            def _():
                give(base + at_z)

    pltpu.make_async_copy(fields.at[me], returned.at[me], local_sem.at[2]).start()
    finish(2, fields, returned, True, N - 1)

    @pl.loop(0, N, unroll=8)
    def _(k):
        first = returned[wrap(k + N - shifts[0], N), 0].astype(F32)
        second = returned[wrap(k + N - shifts[1], N), 1].astype(F32)
        resorted[k] = (first + second).astype(BF16)

    place = 4 * chunk + 2 * lax.rem(me, 2) + core

    def deliver(chip):
        remote(
            resorted.at[chip], arrived.at[place], send_sem.at[3], recv_sem.at[3], chip, plane
        ).start()

    far_first(deliver)

    def sent(phase, buffer, count):
        part = buffer.at[pl.ds(0, count)]
        remote(part, part, send_sem.at[phase], recv_sem.at[phase], me, core).wait_send()

    def close(count):
        both = remote(
            resorted.at[pl.ds(0, count)], arrived.at[pl.ds(0, count)],
            send_sem.at[3], recv_sem.at[3], me, core,
        )
        sent(0, gathered, count)
        sent(1, outgoing, N - 1)
        sent(2, fields, N - 1)
        both.wait_recv()
        both.wait_send()

    @pl.when(same)
    def _():
        own = pltpu.make_async_copy(resorted.at[me], arrived.at[place], local_sem.at[3])
        own.start()
        own.wait()
        close(N - 1)

    @pl.when(jnp.logical_not(same))
    def _():
        deliver(me)
        close(N)

    for q in range(CHUNKS):
        for h in range(2):
            terms = [arrived[4 * q + 2 * h + i].astype(F32) for i in range(2)]
            o_ref[4 * h : 4 * h + 4, q * 128 : (q + 1) * 128] = terms[0] + terms[1]


def shards(orbitals, screening, pair_k, pair_q, gmap):
    vmem = pl.BlockSpec(memory_space=pltpu.VMEM)
    single = pltpu.VMEM((N, 4, 128), BF16)
    double = pltpu.VMEM((N, 2, 4, 128), BF16)
    dma = pltpu.SemaphoreType.DMA
    field = pl.pallas_call(
        kernel,
        out_shape=jax.ShapeDtypeStruct((8, 4096), F32),
        in_specs=[pl.BlockSpec(memory_space=pltpu.HBM)] * 5,
        out_specs=vmem,
        scratch_shapes=[
            pltpu.SMEM((2, 256), jnp.int32),
            pltpu.SMEM((2,), jnp.int32),
            pltpu.VMEM((8, 128), jnp.int32),
            pltpu.VMEM((8, 4096), BF16),
            pltpu.VMEM((CHUNKS, 2, 4, 128), BF16),
            single,
        ]
        + [double] * 4
        + [single] * 2
        + [
            pltpu.VMEM((NG, 4096), BF16),
            pltpu.VMEM((2, NG, NG), BF16),
            pltpu.VMEM((ROWS, 4096), BF16),
            pltpu.VMEM((ROWS, NG), BF16),
            pltpu.VMEM((ROWS, NG), BF16),
            dma((4,)),
            dma((4,)),
            dma((5,)),
            pltpu.SemaphoreType.REGULAR((3,)),
            dma((4,)),
        ],
        compiler_params=pltpu.CompilerParams(
            collective_id=0, has_side_effects=True, vmem_limit_bytes=67043328
        ),
    )(pair_k.T, pair_q, gmap.reshape(8, 128), orbitals, screening)
    return field[None]


def solution(mesh):
    in_specs = (P("kq", "band", None), P("kq", None, None), P(), P("kq"), P())
    out_specs = P("kq", "band", None)
    return jax.shard_map(shards, mesh=mesh, in_specs=in_specs, out_specs=out_specs, check_vma=False)
```
